512 devices in a mesh: orig: 32 (over z_lo, x, core), dest: 16 (over y, z_hi).
Axes of the slice: x: 4, y: 4, z: 16 (z_hi: 4, z_lo: 4; z = z_hi * 4 + z_lo), core: 2. Of those that a mesh axis runs over, the one named last changes fastest.
Arguments:
- pair_field: bfloat16 [1024, 1024, 128], P('orig', 'dest'), may hold values from -6 to 6
- region_mask: int32 [1024], replicated, may hold values 0 or 1
- region_count: int32 [1], replicated, may hold values from 1 to 1024
- row_query: bfloat16 [1, 128, 128], replicated, may hold values from -17.5 to 17.5, as said below
- row_key: bfloat16 [1, 128, 128], replicated, may hold values from -0.36 to 0.36, as said below
- row_value: bfloat16 [1, 128, 128], replicated, may hold values from -0.5 to 0.5
- row_gate: bfloat16 [1, 128, 128], replicated, may hold values from -0.5 to 0.5
- row_gate_bias: float32 [1, 128], replicated, may hold values from -4 to 4
- row_out: bfloat16 [1, 128, 128], replicated, may hold values from -1.5 to 1.5
- col_query: bfloat16 [1, 128, 128], replicated, may hold values from -17.5 to 17.5, as said below
- col_key: bfloat16 [1, 128, 128], replicated, may hold values from -0.36 to 0.36, as said below
- col_value: bfloat16 [1, 128, 128], replicated, may hold values from -0.5 to 0.5
- col_gate: bfloat16 [1, 128, 128], replicated, may hold values from -0.5 to 0.5
- col_gate_bias: float32 [1, 128], replicated, may hold values from -4 to 4
- col_out: bfloat16 [1, 128, 128], replicated, may hold values from -1.5 to 1.5
Outputs:
- new_pair: bfloat16 [1024, 1024, 128], P('orig', 'dest')
The draws below stay inside these ranges and needn't reach their ends.
Inputs may be any that keep to these rules, and one draw needn't show every extreme that they name: `row_query`: row attention query weights. `row_key`: row attention key weights. `col_query`: column attention query weights. `col_key`: column attention key weights.
All inputs are finite; a program needn't handle non-finite values.
Results may differ from the reference program's by a relative error of at most 0.012.
Values may be sent and summed in bfloat16 or wider, within the bound.
A program may use at most 64 MiB of HBM per device.

```python
import math
import jax
import jax.numpy as jnp
from jax import lax

C = 128
H = 4
LAYERS = 1
REGIONS = 1024


def query_and_key(key, salt_value):
    base_key = jax.random.fold_in(key, salt_value)
    draw_one, draw_two = jax.random.split(base_key)
    key_weight = jnp.clip(jax.random.normal(draw_one, (LAYERS, C, C), jnp.float32), -4.0, 4.0) / math.sqrt(C)
    key_weight = jnp.clip(key_weight, -0.35, 0.35)
    noise_part = jnp.clip(jax.random.normal(draw_two, (LAYERS, C, C), jnp.float32), -4.0, 4.0) / math.sqrt(C)
    query_weight = 2.0 * noise_part
    query_weight = jnp.clip(query_weight, -17.5, 17.5)
    return (query_weight, key_weight)


def draw_row_query(key, part):
    return query_and_key(key, 101)[0].astype(jnp.bfloat16)


def draw_row_key(key, part):
    return query_and_key(key, 101)[1].astype(jnp.bfloat16)


def draw_col_query(key, part):
    return query_and_key(key, 203)[0].astype(jnp.bfloat16)


def draw_col_key(key, part):
    return query_and_key(key, 203)[1].astype(jnp.bfloat16)


def touch_ends(values, key, low, top_value):
    shape = values.shape
    spot = [jax.random.randint(jax.random.fold_in(key, axis), (), 0, shape[axis]) for axis in range(len(shape))]
    values = values.at[tuple(spot)].set(low)
    longest = shape.index(max(shape))
    spot[longest] = (spot[longest] + 1) % shape[longest]
    return values.at[tuple(spot)].set(top_value)


def levels(stream_key, extent, pieces, smallest, high):
    def one(axis_at, shards_of):
        draws = jax.random.uniform(jax.random.fold_in(jax.random.fold_in(stream_key, 6), axis_at), (shards_of,), jnp.float32, smallest / len(pieces), high / len(pieces))
        return jnp.repeat(jnp.exp(draws), extent[axis_at] // shards_of).reshape((-1,) + (1,) * (len(extent) - axis_at - 1))

    gain = one(*pieces[0])
    for cut in pieces[1:]:
        gain = gain * one(*cut)
    return gain


def centred(key, shape, width, most, pieces=(), kind=jnp.bfloat16):
    factor_of = levels(key, shape, pieces, -0.22, 0.18) if pieces else 1.0
    drawn = jax.random.normal(key, shape, jnp.float32) * width * factor_of
    return jnp.minimum(jnp.maximum(drawn, -most), most).astype(kind)


def setup_inputs(seed: int = 0) -> dict:
    splits = jax.random.split(jax.random.key(seed), 16)
    return {
        "pair_field": centred(splits[0], (REGIONS, REGIONS, C), 1.0, 6.0, ((0, 32), (1, 16))),
        "region_mask": touch_ends((jax.random.randint(splits[1], (REGIONS,), 0, 4) < 3).astype(jnp.int32), jax.random.fold_in(splits[1], 1), 0, 1),
        "region_count": jax.random.randint(splits[2], (1,), 1, REGIONS + 1).astype(jnp.int32),
        "row_query": draw_row_query(jax.random.fold_in(splits[15], 71), 0),
        "row_key": draw_row_key(jax.random.fold_in(splits[15], 71), 0),
        "row_value": centred(splits[5], (LAYERS, C, C), C ** -0.5, 0.5),
        "row_gate": centred(splits[6], (LAYERS, C, C), C ** -0.5, 0.5),
        "row_gate_bias": centred(splits[7], (LAYERS, C), 1.0, 4.0, (), jnp.float32),
        "row_out": centred(splits[8], (LAYERS, C, C), (C // 8) ** -0.5, 1.5),
        "col_query": draw_col_query(jax.random.fold_in(splits[15], 71), 0),
        "col_key": draw_col_key(jax.random.fold_in(splits[15], 71), 0),
        "col_value": centred(splits[11], (LAYERS, C, C), C ** -0.5, 0.5),
        "col_gate": centred(splits[12], (LAYERS, C, C), C ** -0.5, 0.5),
        "col_gate_bias": centred(splits[13], (LAYERS, C), 1.0, 4.0, (), jnp.float32),
        "col_out": centred(splits[14], (LAYERS, C, C), (C // 8) ** -0.5, 1.5),
    }


epsilon = 1e-05
masked_score = -1e+30

def normalize(pair_rows):
    widened = pair_rows.astype(jnp.float32)
    centered = widened - lax.optimization_barrier(jnp.mean(widened, axis=-1, keepdims=True))
    variance = lax.optimization_barrier(jnp.mean(centered * centered, axis=-1, keepdims=True))
    return (centered * lax.rsqrt(variance + epsilon)).astype(jnp.bfloat16)

def attend_rows(pair_rows, valid_keys, weights):
    w_query, w_key, w_value, w_gate, gate_bias, w_out = weights
    row_count, key_count, channels = pair_rows.shape
    head_size = channels // H
    normed = normalize(pair_rows)
    flattened = normed.reshape(row_count * key_count, channels)

    def project(weight):
        return jnp.dot(flattened, weight, preferred_element_type=jnp.float32)

    def heads_of(weight):
        return project(weight).astype(jnp.bfloat16).reshape(row_count // 8, 8, key_count, H, head_size)
    queries = heads_of(w_query)
    key_rows = heads_of(w_key)
    value_rows = heads_of(w_value)
    gate_values = jax.nn.sigmoid(project(w_gate) + gate_bias[None, :])

    def one_block(operands):
        block_queries, block_keys, block_values = operands
        scores = jnp.einsum('bqhd,bkhd->bhqk', block_queries.astype(jnp.float32), block_keys.astype(jnp.float32), precision=lax.Precision.HIGHEST) / math.sqrt(head_size)
        scores = jnp.where(valid_keys[None, None, None, :], scores, masked_score)
        maximum = lax.optimization_barrier(jnp.max(scores, axis=3, keepdims=True))
        expanded = jnp.exp(scores - maximum)
        block_weights = (expanded / lax.optimization_barrier(jnp.sum(expanded, axis=3, keepdims=True))).astype(jnp.bfloat16)
        return jnp.einsum('bhqk,bkhd->bqhd', block_weights.astype(jnp.float32), block_values.astype(jnp.float32), precision=lax.Precision.HIGHEST).astype(jnp.bfloat16)
    attended = lax.map(one_block, (queries, key_rows, value_rows)).reshape(row_count * key_count, channels)
    gated = (gate_values * attended.astype(jnp.float32)).astype(jnp.bfloat16)
    update = jnp.dot(gated, w_out, preferred_element_type=jnp.float32).reshape(row_count, key_count, channels)
    return (pair_rows.astype(jnp.float32) + update).astype(jnp.bfloat16)

def reference(pair_field, region_mask, region_count, row_query, row_key, row_value, row_gate, row_gate_bias, row_out, col_query, col_key, col_value, col_gate, col_gate_bias, col_out):
    positions = jnp.arange(REGIONS, dtype=jnp.int32)
    valid_keys = ((region_mask == 1) | (positions == 0)) & (positions < region_count[0])
    current = pair_field
    for layer_index in range(LAYERS):
        row_weights = (row_query[layer_index], row_key[layer_index], row_value[layer_index], row_gate[layer_index], row_gate_bias[layer_index], row_out[layer_index])
        col_weights = (col_query[layer_index], col_key[layer_index], col_value[layer_index], col_gate[layer_index], col_gate_bias[layer_index], col_out[layer_index])
        current = attend_rows(current, valid_keys, row_weights)
        turned = jnp.transpose(current, (1, 0, 2))
        current = jnp.transpose(attend_rows(turned, valid_keys, col_weights), (1, 0, 2))
    return current
```

```python
import math

import jax
import jax.numpy as jnp
from jax import lax
from jax.experimental import pallas as pl
from jax.experimental.pallas import tpu as pltpu
from jax.sharding import Mesh
from jax.sharding import PartitionSpec as P

H = 4
C = 128
D = C // H
SCALE = math.log2(math.e) / math.sqrt(D)
ORIG = ("orig_0", "orig_1", "orig_2")
ORIG_DEST = ("orig_0", "orig_1", "orig_2", "dest")


epsilon = 1e-05
masked_score = -1e30


def items_in_groups(x, axis, split_dim, concat_dim, work, item_dim, out_dim):
    items = jax.tree.leaves(x)[0].shape[item_dim]
    count = 2 if items % 2 == 0 else 1
    finished = []
    for k in range(count):
        group = jax.tree.map(
            lambda a: lax.slice_in_dim(
                a, k * (items // count), (k + 1) * (items // count), axis=item_dim
            ),
            x,
        )
        finished.append(
            work(
                lax.all_to_all(
                    group, axis, split_axis=split_dim, concat_axis=concat_dim, tiled=True
                )
            )
        )
    return jax.tree.map(lambda *parts: jnp.concatenate(parts, axis=out_dim), *finished)


def in_blocks(x, dim, size):
    shape = x.shape
    parts = x.reshape(*shape[:dim], size, shape[dim] // size, *shape[dim + 1 :])
    return jnp.moveaxis(parts, dim, 0)


def laid_out(parts, dim):
    shape = list(parts.shape[1:])
    shape[dim] *= parts.shape[0]
    return jnp.moveaxis(parts, 0, dim).reshape(shape)


def one_exchange(x, axis, axes, splits, concats):
    sizes = [lax.axis_size(a) for a in axes]
    parts = in_blocks(x, splits[0], sizes[0])
    parts = jnp.moveaxis(in_blocks(parts, splits[1] + 1, sizes[1]), 0, 1)
    inside = parts.shape[2:]
    parts = parts.reshape(-1, *inside)
    parts = lax.all_to_all(parts, axis, split_axis=0, concat_axis=0, tiled=True)
    parts = laid_out(parts.reshape(*sizes, *inside), concats[0] + 1)
    return laid_out(parts, concats[1])


def moved_by_axis(parts, axes, order):
    inside = parts.shape[1:]
    whole = parts.reshape(*(lax.axis_size(a) for a in axes), *inside)
    for k in order:
        whole = lax.all_to_all(whole, axes[k], k, k, tiled=True)
    return whole.reshape(-1, *inside)


def core_and_chips(x, groups, order, split_dim, concat_dim):
    size = lax.axis_size(groups[0]) * lax.axis_size(groups[1])
    parts = in_blocks(x, split_dim, size)
    return laid_out(moved_by_axis(parts, groups, order), concat_dim)


def prepare(x, bias, w4_ref, gb_ref, kaug, qaug, vall, gates):
    wide = x.astype(jnp.float32)
    centered = wide - jnp.mean(wide, axis=-1, keepdims=True)
    variance = jnp.mean(centered * centered, axis=-1, keepdims=True)
    normed = (centered * lax.rsqrt(variance + epsilon)).astype(jnp.bfloat16)
    proj = jnp.dot(normed, w4_ref[...], preferred_element_type=jnp.float32)
    q = proj[:, :C].astype(jnp.bfloat16).astype(jnp.float32) * SCALE
    high = q.astype(jnp.bfloat16)
    low = (q - high.astype(jnp.float32)).astype(jnp.bfloat16)
    k = proj[:, C : 2 * C].astype(jnp.bfloat16)
    v = proj[:, 2 * C : 3 * C].astype(jnp.bfloat16)
    gates[...] = jax.nn.sigmoid(proj[:, 3 * C :] + gb_ref[...])
    n = x.shape[0]
    lane = lax.broadcasted_iota(jnp.int32, (n, C), 1)
    zero = jnp.zeros((n, C), jnp.bfloat16)
    one = jnp.ones((n, C), jnp.bfloat16)
    for h in range(H):
        mine = (lane >= D * h) & (lane < D * h + D)
        spot = lane == (D * h + D) % C
        qaug[h, :, :C] = jnp.where(mine, high, zero)
        qaug[h, :, C:] = jnp.where(spot, one, jnp.where(mine, low, zero))
        kaug[h, :, :C] = k
        kaug[h, :, C:] = jnp.where(spot, bias, k)
    vall[...] = v


def attend_item(x, kaug, qaug, vall, gates, wo_ref):
    heads = []
    for h in range(H):
        s = lax.dot_general(
            kaug[h], qaug[h], (((1,), (1,)), ((), ())), preferred_element_type=jnp.float32
        )
        p = jnp.exp2(s - jnp.max(s, axis=0, keepdims=True))
        w = (p * (1.0 / jnp.sum(p, axis=0, keepdims=True))).astype(jnp.bfloat16)
        heads.append(
            lax.dot_general(
                vall[:, D * h : D * h + D],
                w,
                (((0,), (0,)), ((), ())),
                preferred_element_type=jnp.float32,
            )
        )
    attended = jnp.concatenate(heads, axis=0).T.astype(jnp.bfloat16).astype(jnp.float32)
    gated = (gates[...] * attended).astype(jnp.bfloat16)
    update = jnp.dot(gated, wo_ref[...], preferred_element_type=jnp.float32)
    return (x.astype(jnp.float32) + update).astype(jnp.bfloat16)


def attend_kernel(x_ref, bias_ref, w4_ref, gb_ref, wo_ref, o_ref, kaug, qaug, vall, gates):
    prepare(x_ref[0], bias_ref[...], w4_ref, gb_ref, kaug, qaug, vall, gates)
    o_ref[0] = attend_item(x_ref[0], kaug, qaug, vall, gates, wo_ref)


def attend_pairs(x, weights, bias):
    w4, gate_bias, w_out = weights
    items, n, c = x.shape

    def whole(a):
        return pl.BlockSpec(a.shape, lambda i: (0,) * a.ndim)

    return pl.pallas_call(
        attend_kernel,
        grid=(items,),
        out_shape=jax.ShapeDtypeStruct(x.shape, jnp.bfloat16),
        in_specs=[
            pl.BlockSpec((1, n, c), lambda i: (i, 0, 0)),
            whole(bias),
            whole(w4),
            whole(gate_bias),
            whole(w_out),
        ],
        out_specs=pl.BlockSpec((1, n, c), lambda i: (i, 0, 0)),
        scratch_shapes=[
            pltpu.VMEM((H, n, 2 * c), jnp.bfloat16),
            pltpu.VMEM((H, n, 2 * c), jnp.bfloat16),
            pltpu.VMEM((n, c), jnp.bfloat16),
            pltpu.VMEM((n, c), jnp.float32),
        ],
        cost_estimate=pl.CostEstimate(
            flops=items * n * n * c * 8, bytes_accessed=items * n * c * 4, transcendentals=items * n * n * H
        ),
    )(x, bias, w4, gate_bias, w_out)


def body(
    pair_field,
    region_mask,
    region_count,
    row_query,
    row_key,
    row_value,
    row_gate,
    row_gate_bias,
    row_out,
    col_query,
    col_key,
    col_value,
    col_gate,
    col_gate_bias,
    col_out,
):
    tile_rows, tile_cols, channels = pair_field.shape
    dest_size = lax.axis_size("dest")
    orig_size = lax.axis_size(ORIG)
    region_total = region_mask.shape[0]
    row_part = tile_rows // dest_size
    col_part = tile_cols // orig_size
    positions = jnp.arange(region_total, dtype=jnp.int32)
    valid_keys = ((region_mask == 1) | (positions == 0)) & (positions < region_count[0])
    current = pair_field
    bias = jnp.broadcast_to(
        jnp.where(valid_keys, 0.0, masked_score).astype(jnp.bfloat16)[:, None],
        (region_total, channels),
    )
    row_weights = (
        jnp.concatenate((row_query[0], row_key[0], row_value[0], row_gate[0]), axis=1),
        row_gate_bias,
        row_out[0],
    )
    col_weights = (
        jnp.concatenate((col_query[0], col_key[0], col_value[0], col_gate[0]), axis=1),
        col_gate_bias,
        col_out[0],
    )

    def row_local(exchanged):
        return attend_pairs(exchanged[0], row_weights, bias)[None]

    pieces = current.reshape(dest_size, row_part, tile_cols, channels)
    rows_whole = items_in_groups(pieces, "dest", 0, 2, row_local, 1, 1)
    spread = rows_whole.reshape(1, 1, row_part, dest_size, orig_size, col_part, channels)
    columns = one_exchange(spread, ORIG_DEST, (ORIG, "dest"), (4, 3), (0, 1))
    column_columns = columns.reshape(region_total, col_part, channels)
    updated = jnp.swapaxes(
        attend_pairs(jnp.swapaxes(column_columns, 0, 1), col_weights, bias), 0, 1
    )
    back = core_and_chips(
        updated.reshape(region_total, 1, col_part, channels),
        (("orig_0", "orig_1"), "orig_2"),
        (1, 0),
        0,
        1,
    )
    current = back.reshape(tile_rows, tile_cols, channels)
    return current


def solution(mesh):
    split = Mesh(
        mesh.devices.reshape(4, 4, 2, mesh.shape["dest"]), ("orig_0", "orig_1", "orig_2", "dest")
    )
    return jax.shard_map(
        body,
        mesh=split,
        in_specs=(
            P(ORIG, "dest", None),
            P(),
            P(),
            P(),
            P(),
            P(),
            P(),
            P(),
            P(),
            P(),
            P(),
            P(),
            P(),
            P(),
            P(),
        ),
        out_specs=P(ORIG, "dest", None),
        check_vma=False,
    )
```

```python
import math

import jax
import jax.numpy as jnp
from jax import lax
from jax.experimental import pallas as pl
from jax.experimental.pallas import tpu as pltpu
from jax.sharding import PartitionSpec as P

H = 4
C = 128
D = C // H
SCALE = math.log2(math.e) / math.sqrt(D)
epsilon = 1e-05
masked_score = -1e30
MESH = pl.DeviceIdType.MESH
BF16 = jnp.bfloat16


def prepare(x, bias, weights, kaug, qaug, vall, gates):
    wq_ref, wk_ref, wv_ref, wg_ref, gb_ref, _ = weights
    wide = x.astype(jnp.float32)
    centered = wide - jnp.mean(wide, axis=-1, keepdims=True)
    variance = jnp.mean(centered * centered, axis=-1, keepdims=True)
    normed = (centered * lax.rsqrt(variance + epsilon)).astype(jnp.bfloat16)

    def project(ref):
        return jnp.dot(normed, ref[...], preferred_element_type=jnp.float32)

    q = project(wq_ref).astype(jnp.bfloat16).astype(jnp.float32) * SCALE
    high = q.astype(jnp.bfloat16)
    low = (q - high.astype(jnp.float32)).astype(jnp.bfloat16)
    k = project(wk_ref).astype(jnp.bfloat16)
    v = project(wv_ref).astype(jnp.bfloat16)
    gates[...] = jax.nn.sigmoid(project(wg_ref) + gb_ref[...])
    n = x.shape[0]
    lane = lax.broadcasted_iota(jnp.int32, (n, C), 1)
    zero = jnp.zeros((n, C), jnp.bfloat16)
    one = jnp.ones((n, C), jnp.bfloat16)
    for h in range(H):
        mine = (lane >= D * h) & (lane < D * h + D)
        spot = lane == (D * h + D) % C
        qaug[h, :, :C] = jnp.where(mine, high, zero)
        qaug[h, :, C:] = jnp.where(spot, one, jnp.where(mine, low, zero))
        kaug[h, :, :C] = k
        kaug[h, :, C:] = jnp.where(spot, bias, k)
    vall[...] = v


def attend_item(x, kaug, qaug, vall, gates, wo_ref):
    heads = []
    for h in range(H):
        s = lax.dot_general(
            kaug[h], qaug[h], (((1,), (1,)), ((), ())), preferred_element_type=jnp.float32
        )
        p = jnp.exp2(s - jnp.max(s, axis=0, keepdims=True))
        w = (p * (1.0 / jnp.sum(p, axis=0, keepdims=True))).astype(jnp.bfloat16)
        heads.append(
            lax.dot_general(
                vall[:, D * h : D * h + D],
                w,
                (((0,), (0,)), ((), ())),
                preferred_element_type=jnp.float32,
            )
        )
    attended = jnp.concatenate(heads, axis=0).T.astype(jnp.bfloat16).astype(jnp.float32)
    gated = (gates[...] * attended).astype(jnp.bfloat16)
    update = jnp.dot(gated, wo_ref[...], preferred_element_type=jnp.float32)
    return (x.astype(jnp.float32) + update).astype(jnp.bfloat16)


def column_of(row):
    ones = jnp.ones((8, C), jnp.float32).astype(BF16)
    first = lax.broadcasted_iota(jnp.int32, (8, row.shape[1]), 0) == 0
    rows = jnp.where(first, jnp.broadcast_to(row, (8, row.shape[1])), 0.0).astype(BF16)
    return lax.dot_general(
        rows, ones, (((0,), (0,)), ((), ())), preferred_element_type=jnp.float32
    ).astype(BF16)


def permuted(matrix, x):
    return jnp.dot(matrix, x, preferred_element_type=jnp.float32).astype(BF16)


def whole_kernel(
    x_ref,
    mask_ref,
    count_ref,
    wq1,
    wk1,
    wv1,
    wg1,
    gb1,
    wo1,
    wq2,
    wk2,
    wv2,
    wg2,
    gb2,
    wo2,
    out_ref,
    rowbuf,
    rowres,
    zbuf,
    turned,
    colbuf,
    colres,
    homebuf,
    kaug,
    qaug,
    vall,
    gates,
    bias,
    swap,
    regroup,
    send_sem,
    recv_sem,
):
    o = lax.axis_index("orig")
    d = lax.axis_index("dest")
    zl, xc = o // 8, o % 8
    y, zh = d // 4, d % 4
    z = zh * 4 + zl
    across = (o + 16) % 32
    plane = xc * 4 + y

    def z_peer(t):
        zz = (z + t) % 16
        return (zz % 4) * 8 + xc, y * 4 + zz // 4

    def plane_peer(t):
        pp = (plane + t) % 32
        return zl * 8 + pp // 4, (pp % 4) * 4 + zh

    def home_peer(t):
        return (o + t) % 32, d

    barrier = pltpu.get_barrier_semaphore()

    def greet(peer, first, last):
        @pl.loop(first, last)
        def _(t):
            pl.semaphore_signal(barrier, inc=1, device_id=peer(t), device_id_type=MESH)

    greet(lambda t: (across, (d + t) % 16), 0, 16)
    greet(z_peer, 1, 16)
    greet(plane_peer, 1, 32)
    greet(home_peer, 1, 32)

    valid_row = (mask_ref[0:1] == 1) | (lax.broadcasted_iota(jnp.int32, (1, 1024), 1) == 0)
    valid_row = valid_row & (lax.broadcasted_iota(jnp.int32, (1, 1024), 1) < count_ref[0])
    bias[0] = column_of(jnp.where(valid_row, 0.0, masked_score))
    valid_col = (mask_ref[1:2] == 1) | (mask_ref[2:3] == 0)
    valid_col = valid_col & (mask_ref[2:3] < count_ref[0])
    bias[1] = column_of(jnp.where(valid_col, 0.0, masked_score))
    to = lax.broadcasted_iota(jnp.int32, (256, 256), 0)
    source = lax.broadcasted_iota(jnp.int32, (256, 256), 1)
    swap[...] = jnp.where(source == (to & 15) * 16 + (to >> 4), 1.0, 0.0).astype(BF16)
    regroup[...] = jnp.where(
        source == (to & 192) + ((to >> 2) & 3) * 16 + ((to >> 4) & 3) * 4 + (to & 3), 1.0, 0.0
    ).astype(BF16)

    pl.semaphore_wait(barrier, 16 + 15 + 31 + 31)

    def put(src, dst, stage, part, peer):
        pltpu.make_async_remote_copy(
            src_ref=src,
            dst_ref=dst,
            send_sem=send_sem.at[stage, part],
            recv_sem=recv_sem.at[stage, part],
            device_id=peer,
            device_id_type=MESH,
        ).start()

    def waiting(ref, stage, part):
        return pltpu.make_async_remote_copy(
            src_ref=ref,
            dst_ref=ref,
            send_sem=send_sem.at[stage, part],
            recv_sem=recv_sem.at[stage, part],
            device_id=(across, d),
            device_id_type=MESH,
        )

    def outwards(t):
        return 8 + ((t + 1) // 2) * (1 - 2 * (t % 2))

    for r in range(2):

        @pl.loop(0, 16)
        def _(t):
            to_d = (d + t) % 16
            put(x_ref.at[to_d, r], rowbuf.at[r, d], 0, r, (across, to_d))

    @pl.loop(0, 2)
    def _(r):
        waiting(rowbuf.at[r], 0, r).wait_recv()
        x = rowbuf[r].reshape(1024, C)
        prepare(x, bias[0], (wq1, wk1, wv1, wg1, gb1, wo1), kaug, qaug, vall, gates)
        rowres[r] = attend_item(x, kaug, qaug, vall, gates, wo1).reshape(4, 4, 4, 16, C)

        @pl.loop(0, 15)
        def _(t):
            zz = (z + outwards(t)) % 16
            put(
                rowres.at[r, :, zz // 4, zz % 4],
                zbuf.at[r, :, zl * 4 + zh],
                1,
                r,
                ((zz % 4) * 8 + xc, y * 4 + zz // 4),
            )

        zbuf[r, :, zl * 4 + zh] = rowres[r, :, zh, zl]

    @pl.loop(0, 2)
    def _(r):
        waiting(zbuf.at[r, :, 0:15], 1, r).wait_recv()
        for yy in range(4):
            turned[r, yy] = permuted(swap[...], zbuf[r, yy].reshape(256, C)).reshape(8, 2, 16, C)

        @pl.loop(1, 32)
        def _(t):
            pp = (plane + t) % 32
            put(
                turned.at[r, pp % 4, pp // 4],
                colbuf.at[:, r, plane],
                2,
                r,
                (zl * 8 + pp // 4, (pp % 4) * 4 + zh),
            )

        colbuf[:, r, plane] = turned[r, y, xc]

    for r in range(2):
        waiting(colbuf.at[:, r, 0:31], 2, r).wait_recv()

    @pl.loop(0, 2)
    def _(b):
        x = colbuf[b].reshape(1024, C)
        prepare(x, bias[1], (wq2, wk2, wv2, wg2, gb2, wo2), kaug, qaug, vall, gates)
        done = attend_item(x, kaug, qaug, vall, gates, wo2)
        for part in range(4):
            colres[b, part // 2, 4 * (part % 2) : 4 * (part % 2) + 4] = permuted(
                regroup[...], done[256 * part : 256 * part + 256]
            ).reshape(4, 4, 16, C)

        @pl.loop(1, 32)
        def _(t):
            oo = (o + t) % 32
            put(
                colres.at[b, :, oo % 8, (oo // 8 + 2) % 4],
                homebuf.at[:, o, b],
                3,
                b,
                (oo, d),
            )

        homebuf[:, o, b] = colres[b, :, xc, (zl + 2) % 4]

    for b in range(2):
        waiting(homebuf.at[:, 0:31, b], 3, b).wait_recv()
    for r in range(2):
        for q in range(4):
            out_ref[:, r, 16 * q : 16 * q + 16] = permuted(
                swap[...], homebuf[r, 8 * q : 8 * q + 8].reshape(256, C)
            ).reshape(16, 16, C)
    for part in range(2):
        waiting(rowbuf.at[part], 0, part).wait_send()
        waiting(zbuf.at[part, :, 0:15], 1, part).wait_send()
        waiting(colbuf.at[:, part, 0:31], 2, part).wait_send()
        waiting(homebuf.at[:, 0:31, part], 3, part).wait_send()


def body(pair_field, region_mask, region_count, *weights):
    weights = [w if w.ndim == 2 else w[0] for w in weights]
    positions = jnp.arange(1024, dtype=jnp.int32)

    def by_column_owner(a):
        parts = a.reshape(4, 8, 4, 4, 2)
        parts = jnp.concatenate((parts[2:], parts[:2]), axis=0)
        return jnp.transpose(parts, (4, 1, 2, 0, 3)).reshape(1024)

    masks = jnp.stack((region_mask, by_column_owner(region_mask), by_column_owner(positions)))
    vmem = pl.BlockSpec(memory_space=pltpu.VMEM)
    out = pl.pallas_call(
        whole_kernel,
        out_shape=jax.ShapeDtypeStruct((16, 2, 64, C), BF16),
        in_specs=[vmem, vmem, pl.BlockSpec(memory_space=pltpu.SMEM)] + [vmem] * 12,
        out_specs=vmem,
        scratch_shapes=[
            pltpu.VMEM((2, 16, 64, C), BF16),
            pltpu.VMEM((2, 4, 4, 4, 16, C), BF16),
            pltpu.VMEM((2, 4, 16, 16, C), BF16),
            pltpu.VMEM((2, 4, 8, 2, 16, C), BF16),
            pltpu.VMEM((2, 2, 32, 16, C), BF16),
            pltpu.VMEM((2, 2, 8, 4, 16, C), BF16),
            pltpu.VMEM((2, 32, 2, 16, C), BF16),
            pltpu.VMEM((H, 1024, 2 * C), BF16),
            pltpu.VMEM((H, 1024, 2 * C), BF16),
            pltpu.VMEM((1024, C), BF16),
            pltpu.VMEM((1024, C), jnp.float32),
            pltpu.VMEM((2, 1024, C), BF16),
            pltpu.VMEM((256, 256), BF16),
            pltpu.VMEM((256, 256), BF16),
            pltpu.SemaphoreType.DMA((4, 2)),
            pltpu.SemaphoreType.DMA((4, 2)),
        ],
        compiler_params=pltpu.CompilerParams(
            collective_id=0, has_side_effects=True, vmem_limit_bytes=60 * 1024 * 1024
        ),
    )(pair_field.reshape(16, 2, 64, C), masks, region_count, *weights)
    return out.reshape(32, 64, C)


def solution(mesh):
    tile = P("orig", "dest", None)
    return jax.shard_map(
        body,
        mesh=mesh,
        in_specs=(tile,) + (P(),) * 14,
        out_specs=tile,
        check_vma=False,
    )
```
